32 devices in a mesh: slab: 16 (over z, y, x), energy: 2 (over core).
Axes of the slice: x: 2, y: 2, z: 4, core: 2. Of those that a mesh axis runs over, the one named last changes fastest.
Arguments:
- onsite_energy: float32 [32, 128], P('slab'), may hold values from -0.3 to 0.3
- onsite_mixing: float32 [32, 128, 128], P('slab'), may hold values from -0.15625 to 0.15625
- hop_strength: float32 [32, 128], P('slab'), may hold values from 0.8 to 1.2
- hop_mixing: float32 [32, 128, 128], P('slab'), may hold values from -0.15625 to 0.15625
- energy: float32 [2], P('energy'), parts along dimension 0, may hold values from -0.4 to 0.4
- broadening: float32 [2], P('energy'), parts along dimension 0, may hold values from 0.01 to 0.025
Outputs:
- green_real: float32 [64, 128, 128], P(('energy', 'slab')), parts along dimension 0
- green_imag: float32 [64, 128, 128], P(('energy', 'slab')), parts along dimension 0
The draws below stay inside these ranges and needn't reach their ends.
There are 2 independent parts, one for each index of `energy`. The reference program is written for one: setup_inputs(seed, part) draws one part's arguments, and reference() takes and returns one part's arrays. A program takes and returns all parts, laid end to end along the dimension named above; an argument that names none is the same for every part. Nothing has to cross between parts.
All inputs are finite; a program needn't handle non-finite values.
Results may differ from the reference program's by a relative error of at most 0.0007.
Values sent between devices are 32-bit elements; how exact they have to be, the bound alone decides.
No kernel may reach another device: no remote copies, remote signals or barrier semaphores. Data moves between devices by JAX's collectives and lax.ppermute only.
A program may use at most 128 MiB of HBM per device.

```python
import math
import jax
import jax.numpy as jnp
from jax import lax

ORB = 128
SLABS = 32


def steps_of(own_key, extent, cuts, smallest, largest):
    loudness = 1.0
    for position, shards_of in cuts:
        heights = jax.random.uniform(jax.random.fold_in(jax.random.fold_in(own_key, 6), position), (shards_of,), jnp.float32, smallest / len(cuts), largest / len(cuts))
        loudness = loudness * jnp.repeat(jnp.exp(heights), extent[position] // shards_of).reshape((-1,) + (1,) * (len(extent) - 1 - position))
    return loudness


def centred(rng, shape, scale, bound, pieces=(), kind=jnp.bfloat16):
    drawn = jax.random.normal(rng, shape, jnp.float32) * scale
    if len(pieces) > 0:
        drawn = steps_of(rng, shape, pieces, -0.22, 0.18) * drawn
    return jnp.clip(drawn, min=-bound, max=bound).astype(kind)


def setup_inputs(seed: int = 0, part: int = 0) -> dict:
    seeds = jax.random.split(jax.random.key(seed), 7)
    own_keys = jax.random.split(jax.random.fold_in(seeds[6], part), 7)
    onsite_energy = jnp.clip(jax.random.uniform(seeds[0], (SLABS, ORB), jnp.float32, -0.3, 0.3) * steps_of(seeds[0], (SLABS, ORB), ((0, 16),), -0.4, 0.0), -0.3, 0.3)
    onsite_mixing = centred(seeds[1], (SLABS, ORB, ORB), (10 * ORB) ** -0.5, 0.15625, ((0, 16),), jnp.float32)
    hop_strength = jnp.clip(0.8 + 0.40000004 * jax.random.uniform(seeds[2], (SLABS, ORB), jnp.float32) ** steps_of(seeds[2], (SLABS, ORB), ((0, 16),), -0.2, 0.2), 0.8, 1.2)
    hop_mixing = centred(seeds[3], (SLABS, ORB, ORB), (10 * ORB) ** -0.5, 0.15625, ((0, 16),), jnp.float32)
    energy = jnp.clip(jax.random.uniform(own_keys[4], (1,), jnp.float32, -0.4, 0.4), -0.4, 0.4)
    broadening = jnp.clip(jnp.exp(jax.random.uniform(own_keys[5], (1,), jnp.float32, math.log(0.01), math.log(0.025))), 0.01, 0.025)
    return dict(onsite_energy=onsite_energy, onsite_mixing=onsite_mixing, hop_strength=hop_strength, hop_mixing=hop_mixing, energy=energy, broadening=broadening)


def real_product(first, second):
    return jnp.dot(first.astype(jnp.float32), second.astype(jnp.float32), precision=lax.Precision.HIGHEST, preferred_element_type=jnp.float32)

def complex_product(first, second):
    return (real_product(first[0], second[0]) - real_product(first[1], second[1]), real_product(first[0], second[1]) + real_product(first[1], second[0]))

def invert_exact(real_part, imag_part):
    orbitals = real_part.shape[0]
    stacked = jnp.concatenate([jnp.concatenate([real_part, -imag_part], axis=1), jnp.concatenate([imag_part, real_part], axis=1)], axis=0)
    whole = jnp.linalg.inv(stacked)
    return (whole[:orbitals, :orbitals], whole[orbitals:, :orbitals])

def reference(onsite_energy, onsite_mixing, hop_strength, hop_mixing, energy, broadening):
    orbitals = onsite_mixing.shape[1]
    identity = jnp.eye(orbitals, dtype=jnp.float32)
    hamilton = jax.vmap(jnp.diag)(onsite_energy) + 0.5 * (onsite_mixing + jnp.swapaxes(onsite_mixing, 1, 2))
    diagonal_real = energy[0] * identity - hamilton
    diagonal_imag = broadening[0] * identity
    couplings = jax.vmap(jnp.diag)(hop_strength) + hop_mixing
    empty_block = jnp.zeros((orbitals, orbitals), jnp.float32)

    def sweep_forward(carried, inputs):
        previous_real, previous_imag, coupling = carried
        block_real, next_coupling = inputs
        reduced_real = block_real - real_product(real_product(coupling.T, previous_real), coupling)
        reduced_imag = diagonal_imag - real_product(real_product(coupling.T, previous_imag), coupling)
        connected = invert_exact(reduced_real, reduced_imag)
        return ((connected[0], connected[1], next_coupling), connected)
    ending, connected = lax.scan(sweep_forward, (empty_block, empty_block, empty_block), (diagonal_real, couplings))

    def sweep_backward(following, inputs):
        here_real, here_imag, coupling = inputs
        left_side = (real_product(here_real, coupling), real_product(here_imag, coupling))
        middle = complex_product(left_side, following)
        right_side = (real_product(middle[0], coupling.T), real_product(middle[1], coupling.T))
        correction = complex_product(right_side, (here_real, here_imag))
        result = (here_real + correction[0], here_imag + correction[1])
        return (result, result)
    final_block = (connected[0][-1], connected[1][-1])
    leftover, earlier = lax.scan(sweep_backward, final_block, (connected[0][:-1], connected[1][:-1], couplings[:-1]), reverse=True)
    green_real = jnp.concatenate([earlier[0], final_block[0][None]], axis=0)
    green_imag = jnp.concatenate([earlier[1], final_block[1][None]], axis=0)
    return (green_real, green_imag)
```

```python
import jax
import jax.numpy as jnp
from jax import lax
from jax.experimental import pallas as pl
from jax.experimental.pallas import tpu as pltpu
from jax.sharding import PartitionSpec as P

PANEL = 8
REFINE = 2


def passed_along(block, axis, distance):
    devices = range(lax.axis_size(axis))
    route = [(i - distance, i) for i in devices if i - distance in devices]
    return lax.ppermute(block, axis, route)


def split3(x):
    first = x.astype(jnp.bfloat16)
    rest = x - first.astype(jnp.float32)
    second = rest.astype(jnp.bfloat16)
    third = (rest - second.astype(jnp.float32)).astype(jnp.bfloat16)
    return first, second, third


def halves(wide):
    n = wide.shape[0]
    return wide[:, :n], wide[:, n:]


def right_factor(wide):
    re, im = halves(wide)
    return jnp.concatenate(
        [jnp.concatenate([re, im], axis=1), jnp.concatenate([-im, re], axis=1)], axis=0
    )


def right_factor_t(wide):
    re, im = halves(wide)
    return jnp.concatenate(
        [jnp.concatenate([re, -im], axis=1), jnp.concatenate([im, re], axis=1)], axis=0
    )


def times(first, second):
    return jnp.dot(
        first, right_factor(second), precision=lax.Precision.HIGHEST,
        preferred_element_type=jnp.float32,
    )


def times_t(first, second):
    return lax.dot_general(
        first, right_factor_t(second), (((1,), (1,)), ((), ())),
        precision=lax.Precision.HIGHEST, preferred_element_type=jnp.float32,
    )


def panel_factors(rows, start, n):
    re, im = rows[:, :n], rows[:, n:]
    b = rows.shape[0]
    sub = lax.broadcasted_iota(jnp.int32, (b, n), 0)
    lane = lax.broadcasted_iota(jnp.int32, (b, n), 1)
    v_re = re - jnp.where(lane == sub + start, 1.0, 0.0)
    v_im = im
    cols = [
        (
            jnp.broadcast_to(re[:, start + k : start + k + 1], (b, n)),
            jnp.broadcast_to(im[:, start + k : start + k + 1], (b, n)),
        )
        for k in range(b)
    ]
    cols.append((v_re, v_im))
    for j in range(b):
        c_re, c_im = cols[j]
        p_re, p_im = c_re[j : j + 1], c_im[j : j + 1]
        scale = 1.0 / (p_re * p_re + p_im * p_im)
        q_re, q_im = p_re * scale, -p_im * scale
        for k in range(j + 1, b + 1):
            m_re, m_im = cols[k]
            r_re, r_im = m_re[j : j + 1], m_im[j : j + 1]
            t_re = jnp.broadcast_to(r_re * q_re - r_im * q_im, (b, n))
            t_im = jnp.broadcast_to(r_re * q_im + r_im * q_re, (b, n))
            cols[k] = (
                jnp.where(sub == j, t_re, m_re - (c_re * t_re - c_im * t_im)),
                jnp.where(sub == j, t_im, m_im - (c_re * t_im + c_im * t_re)),
            )
    return (v_re, v_im), cols[b]


def rank_update(v, p):
    lhs = jnp.concatenate([v[0], v[1]], axis=0)
    rhs = jnp.concatenate(
        [jnp.concatenate([p[0], p[1]], axis=1), jnp.concatenate([-p[1], p[0]], axis=1)], axis=0
    )
    a1, a2, a3 = split3(lhs)
    b1, b2, b3 = split3(rhs)
    return lax.dot_general(
        jnp.concatenate([a1, a1, a2, a2, a1, a3], axis=0),
        jnp.concatenate([b1, b2, b1, b2, b3, b1], axis=0),
        (((0,), (0,)), ((), ())),
        preferred_element_type=jnp.float32,
    )


def invert_body(d_ref, x_ref, work):
    count, n, wide = d_ref.shape
    row = lax.broadcasted_iota(jnp.int32, (n, wide), 0)
    col = lax.broadcasted_iota(jnp.int32, (n, wide), 1)
    two = jnp.where(row == col, 2.0, 0.0)
    for s in range(count):
        work[s] = d_ref[s]
    for start in range(0, n, PANEL):
        factors = [panel_factors(work[s, start : start + PANEL, :], start, n) for s in range(count)]
        for s in range(count):
            work[s] = work[s] - rank_update(*factors[s])
    results = [two - work[s] for s in range(count)]
    for _ in range(REFINE):
        steps = [two - times(d_ref[s], results[s]) for s in range(count)]
        results = [times(results[s], steps[s]) for s in range(count)]
    for s in range(count):
        x_ref[s] = results[s]


def invert(d):
    return pl.pallas_call(
        invert_body,
        out_shape=jax.ShapeDtypeStruct(d.shape, jnp.float32),
        scratch_shapes=[pltpu.VMEM(d.shape, jnp.float32)],
        name="invert",
    )(d)


def update_body(links, d, l, r, x_low, x_high, *rest):
    if links:
        l_low, r_high, d_out, l_out, r_out = rest
    else:
        (d_out,) = rest
    for s in range(d.shape[0]):
        low = times(l[s], x_low[s])
        high = times(r[s], x_high[s])
        d_out[s] = d[s] - times_t(low, l[s]) - times_t(high, r[s])
        if links:
            l_out[s] = -times(low, l_low[s])
            r_out[s] = -times(high, r_high[s])


def update(links, *operands):
    shape = jax.ShapeDtypeStruct(operands[0].shape, jnp.float32)
    return pl.pallas_call(
        lambda *refs: update_body(links, *refs),
        out_shape=(shape,) * (3 if links else 1),
        name="update",
    )(*operands)


def shards(onsite_energy, onsite_mixing, hop_strength, hop_mixing, energy, broadening):
    orbitals = onsite_mixing.shape[1]
    device_count = lax.axis_size("slab")
    level_count = device_count.bit_length() - 1
    position = lax.axis_index("slab")
    identity = jnp.eye(orbitals, dtype=jnp.float32)

    def widened(real):
        return jnp.concatenate([real, jnp.zeros_like(real)], axis=-1)

    mixing = 0.5 * (onsite_mixing + jnp.swapaxes(onsite_mixing, 1, 2))
    d = jnp.concatenate(
        [
            energy[0] * identity - (onsite_energy[:, :, None] * identity + mixing),
            jnp.broadcast_to(broadening[0] * identity, mixing.shape),
        ],
        axis=-1,
    )
    hop = -(hop_strength[:, :, None] * identity + hop_mixing)
    last = (position == device_count - 1) & (jnp.arange(2)[:, None, None] == 1)
    hop = jnp.where(last, 0.0, hop)
    hop_below = passed_along(hop, "slab", 1)
    hop_above = passed_along(hop[0], "slab", -1)
    x = invert(d)
    x_below = passed_along(x[1], "slab", 1)
    x_above = passed_along(x[0], "slab", -1)
    l = widened(jnp.stack([hop_below[1].T, hop[0].T]))
    r = widened(hop)
    l_low = widened(jnp.stack([hop_below[0].T, hop_below[1].T]))
    r_high = widened(jnp.stack([hop[1], hop_above]))
    d, l, r = update(
        True, d, l, r, jnp.stack([x_below, x[0]]), jnp.stack([x[1], x_above]), l_low, r_high
    )
    for level in range(level_count):
        stride = 1 << level
        links = level < level_count - 1
        if links:
            l_low = passed_along(l, "slab", stride)
            r_high = passed_along(r, "slab", -stride)
        x = invert(d)
        x_low = passed_along(x, "slab", stride)
        x_high = passed_along(x, "slab", -stride)
        if links:
            d, l, r = update(True, d, l, r, x_low, x_high, l_low, r_high)
        else:
            (d,) = update(False, d, l, r, x_low, x_high)
    g = invert(d)
    return g[:, :, :orbitals], g[:, :, orbitals:]


def solution(mesh):
    return jax.shard_map(
        shards,
        mesh=mesh,
        in_specs=(
            P("slab", None),
            P("slab", None, None),
            P("slab", None),
            P("slab", None, None),
            P("energy"),
            P("energy"),
        ),
        out_specs=(P(("energy", "slab"), None, None), P(("energy", "slab"), None, None)),
        check_vma=False,
    )
```

```python
import jax
import jax.numpy as jnp
from jax import lax
from jax.experimental import pallas as pl
from jax.experimental.pallas import tpu as pltpu
from jax.sharding import PartitionSpec as P

PANEL = 8


def passed_along(block, axis, distance):
    devices = range(lax.axis_size(axis))
    route = [(i - distance, i) for i in devices if i - distance in devices]
    return lax.ppermute(block, axis, route)


def split3(x):
    first = x.astype(jnp.bfloat16)
    rest = x - first.astype(jnp.float32)
    second = rest.astype(jnp.bfloat16)
    third = (rest - second.astype(jnp.float32)).astype(jnp.bfloat16)
    return first, second, third


def halves(wide):
    n = wide.shape[0]
    return wide[:, :n], wide[:, n:]


def right_factor(wide):
    re, im = halves(wide)
    return jnp.concatenate(
        [jnp.concatenate([re, im], axis=1), jnp.concatenate([-im, re], axis=1)], axis=0
    )


def right_factor_t(wide):
    re, im = halves(wide)
    return jnp.concatenate(
        [jnp.concatenate([re, -im], axis=1), jnp.concatenate([im, re], axis=1)], axis=0
    )


def times(first, second):
    return jnp.dot(
        first, right_factor(second), precision=lax.Precision.HIGHEST,
        preferred_element_type=jnp.float32,
    )


def times_t(first, second):
    return lax.dot_general(
        first, right_factor_t(second), (((1,), (1,)), ((), ())),
        precision=lax.Precision.HIGHEST, preferred_element_type=jnp.float32,
    )


def panel_factors(rows, start, n):
    re, im = rows[:, :n], rows[:, n:]
    b = rows.shape[0]
    sub = lax.broadcasted_iota(jnp.int32, (b, n), 0)
    lane = lax.broadcasted_iota(jnp.int32, (b, n), 1)
    v_re = re - jnp.where(lane == sub + start, 1.0, 0.0)
    v_im = im
    cols = [
        (
            jnp.broadcast_to(re[:, start + k : start + k + 1], (b, n)),
            jnp.broadcast_to(im[:, start + k : start + k + 1], (b, n)),
        )
        for k in range(b)
    ]
    cols.append((v_re, v_im))
    for j in range(b):
        c_re, c_im = cols[j]
        p_re, p_im = c_re[j : j + 1], c_im[j : j + 1]
        scale = 1.0 / (p_re * p_re + p_im * p_im)
        q_re, q_im = p_re * scale, -p_im * scale
        for k in range(j + 1, b + 1):
            m_re, m_im = cols[k]
            r_re, r_im = m_re[j : j + 1], m_im[j : j + 1]
            t_re = jnp.broadcast_to(r_re * q_re - r_im * q_im, (b, n))
            t_im = jnp.broadcast_to(r_re * q_im + r_im * q_re, (b, n))
            cols[k] = (
                jnp.where(sub == j, t_re, m_re - (c_re * t_re - c_im * t_im)),
                jnp.where(sub == j, t_im, m_im - (c_re * t_im + c_im * t_re)),
            )
    return (v_re, v_im), cols[b]


def rank_update(v, p):
    lhs = jnp.concatenate([v[0], v[1]], axis=0)
    rhs = jnp.concatenate(
        [jnp.concatenate([p[0], p[1]], axis=1), jnp.concatenate([-p[1], p[0]], axis=1)], axis=0
    )
    a1, a2, a3 = split3(lhs)
    b1, b2, b3 = split3(rhs)
    return lax.dot_general(
        jnp.concatenate([a1, a1, a2, a2, a1, a3], axis=0),
        jnp.concatenate([b1, b2, b1, b2, b3, b1], axis=0),
        (((0,), (0,)), ((), ())),
        preferred_element_type=jnp.float32,
    )


def masks(n):
    row = lax.broadcasted_iota(jnp.int32, (n, n), 0)
    col = lax.broadcasted_iota(jnp.int32, (n, n), 1)
    return row, col


def sweep(blocks, work):
    count = len(blocks)
    n, wide = blocks[0].shape
    row = lax.broadcasted_iota(jnp.int32, (n, wide), 0)
    col = lax.broadcasted_iota(jnp.int32, (n, wide), 1)
    two = jnp.where(row == col, 2.0, 0.0)
    for s in range(count):
        work[s] = blocks[s]
    for start in range(0, n, PANEL):
        factors = [panel_factors(work[s, start : start + PANEL, :], start, n) for s in range(count)]
        for s in range(count):
            work[s] = work[s] - rank_update(*factors[s])
    return [two - work[s] for s in range(count)]


def refined(block, estimate):
    n, wide = block.shape
    row = lax.broadcasted_iota(jnp.int32, (n, wide), 0)
    col = lax.broadcasted_iota(jnp.int32, (n, wide), 1)
    two = jnp.where(row == col, 2.0, 0.0)
    return times(estimate, two - times(block, estimate))


def store_packed(out, wide):
    re, im = halves(wide)
    n = re.shape[0]
    row, col = masks(n)
    out[:n, :] = jnp.where(col >= row, re, im)
    diagonal = jnp.sum(jnp.where(col == row, im, 0.0), axis=0, keepdims=True)
    out[n:, :] = jnp.broadcast_to(diagonal, (PANEL, n))


def unpacked(packed):
    n = packed.shape[1]
    row, col = masks(n)
    body = packed[:n, :]
    turned = body.T
    re = jnp.where(col >= row, body, turned)
    im = jnp.where(col < row, body, turned)
    im = jnp.where(col == row, packed[n : n + 1, :], im)
    return jnp.concatenate([re, im], axis=1)


def symmetric(wide):
    re, im = halves(wide)
    return jnp.concatenate([0.5 * (re + re.T), 0.5 * (im + im.T)], axis=1)


def first_body(energy, broadening, onsite_energy, mixing, d_out, low_out, high_out, work):
    count, n, _ = mixing.shape
    row, col = masks(n)
    blocks = []
    for s in range(count):
        m = mixing[s]
        re = jnp.where(row == col, energy[0] - onsite_energy[s : s + 1, :], 0.0) - 0.5 * (m + m.T)
        im = jnp.where(row == col, broadening[0], 0.0)
        blocks.append(jnp.concatenate([re, im], axis=1))
        d_out[s] = blocks[s]
    found = sweep(blocks, work)
    for s, out in enumerate((low_out, high_out)):
        store_packed(out, refined(d_out[s], found[s]))


def first(energy, broadening, onsite_energy, mixing):
    count, n, _ = mixing.shape
    packed = jax.ShapeDtypeStruct((n + PANEL, n), jnp.float32)
    whole = pl.BlockSpec(memory_space=pltpu.VMEM)
    scalar = pl.BlockSpec(memory_space=pltpu.SMEM)
    return pl.pallas_call(
        first_body,
        in_specs=[scalar, scalar, whole, whole],
        out_shape=(jax.ShapeDtypeStruct((count, n, 2 * n), jnp.float32), packed, packed),
        scratch_shapes=[pltpu.VMEM((count, n, 2 * n), jnp.float32)],
        name="first",
    )(energy, broadening, onsite_energy, mixing)


def invert_body(d_ref, x_ref, work):
    count = d_ref.shape[0]
    found = sweep([d_ref[s] for s in range(count)], work)
    for s in range(count):
        store_packed(x_ref.at[s], refined(d_ref[s], found[s]))


def invert(d):
    count, n, _ = d.shape
    return pl.pallas_call(
        invert_body,
        out_shape=jax.ShapeDtypeStruct((count, n + PANEL, n), jnp.float32),
        scratch_shapes=[pltpu.VMEM(d.shape, jnp.float32)],
        name="invert",
    )(d)


def dot32(first, second, dims):
    return lax.dot_general(
        first, second, (dims, ((), ())), precision=lax.Precision.HIGHEST,
        preferred_element_type=jnp.float32,
    )


def update_first_body(d, hop, below, above, own_low, own_high, x_below, x_above, d_out, l_out, r_out):
    n = hop.shape[1]
    own_low, own_high = unpacked(own_low[...]), unpacked(own_high[...])
    x_below, x_above = unpacked(x_below[...]), unpacked(x_above[...])
    plan = (
        (below[1], below[0], x_below, hop[0], hop[1], own_high),
        (hop[0], below[1], own_low, hop[1], above[...], x_above),
    )
    for s, (t_low, t_lower, x_low, t_high, t_higher, x_high) in enumerate(plan):
        low = dot32(t_low, x_low, ((0,), (0,)))
        high = dot32(t_high, x_high, ((1,), (0,)))
        low_re, low_im = halves(low)
        high_re, high_im = halves(high)
        tall_low = jnp.concatenate([low_re, low_im], axis=0)
        tall_high = jnp.concatenate([high_re, high_im], axis=0)
        shift = dot32(tall_low, t_low, ((1,), (0,))) + dot32(tall_high, t_high, ((1,), (1,)))
        d_out[s] = symmetric(d[s] - jnp.concatenate([shift[:n], shift[n:]], axis=1))
        link_low = -dot32(tall_low, t_lower, ((1,), (1,)))
        link_high = -dot32(tall_high, t_higher, ((1,), (0,)))
        l_out[s] = jnp.concatenate([link_low[:n], link_low[n:]], axis=1)
        r_out[s] = jnp.concatenate([link_high[:n], link_high[n:]], axis=1)


def update_first(*operands):
    shape = jax.ShapeDtypeStruct(operands[0].shape, jnp.float32)
    return pl.pallas_call(update_first_body, out_shape=(shape,) * 3, name="update_first")(*operands)


def update_body(d, l, r, x_low, x_high, l_low, r_high, d_out, l_out, r_out):
    for s in range(d.shape[0]):
        low = times(l[s], unpacked(x_low[s]))
        high = times(r[s], unpacked(x_high[s]))
        d_out[s] = symmetric(d[s] - times_t(low, l[s]) - times_t(high, r[s]))
        l_out[s] = -times(low, l_low[s])
        r_out[s] = -times(high, r_high[s])


def update(*operands):
    shape = jax.ShapeDtypeStruct(operands[0].shape, jnp.float32)
    return pl.pallas_call(update_body, out_shape=(shape,) * 3, name="update")(*operands)


def last_body(d, l, r, x_low, x_high, re_out, im_out, block, work):
    count = d.shape[0]
    for s in range(count):
        low = times(l[s], unpacked(x_low[s]))
        high = times(r[s], unpacked(x_high[s]))
        block[s] = symmetric(d[s] - times_t(low, l[s]) - times_t(high, r[s]))
    found = sweep([block[s] for s in range(count)], work)
    for s in range(count):
        re_out[s], im_out[s] = halves(refined(block[s], found[s]))


def last(*operands):
    count, n, wide = operands[0].shape
    shape = jax.ShapeDtypeStruct((count, n, n), jnp.float32)
    return pl.pallas_call(
        last_body,
        out_shape=(shape, shape),
        scratch_shapes=[pltpu.VMEM((count, n, wide), jnp.float32)] * 2,
        name="last",
    )(*operands)


def shards(onsite_energy, onsite_mixing, hop_strength, hop_mixing, energy, broadening):
    orbitals = onsite_mixing.shape[1]
    level_count = lax.axis_size("slab").bit_length() - 1
    identity = jnp.eye(orbitals, dtype=jnp.float32)
    hop = hop_strength[:, :, None] * identity + hop_mixing
    below = passed_along(hop, "slab", 1)
    above = passed_along(hop[0], "slab", -1)
    d, x_first, x_second = first(energy, broadening, onsite_energy, onsite_mixing)
    x_below = passed_along(x_second, "slab", 1)
    x_above = passed_along(x_first, "slab", -1)
    d, l, r = update_first(d, hop, below, above, x_first, x_second, x_below, x_above)
    for level in range(level_count):
        stride = 1 << level
        links = level < level_count - 1
        if links:
            l_low = passed_along(l, "slab", stride)
            r_high = passed_along(r, "slab", -stride)
        x = invert(d)
        x_low = passed_along(x, "slab", stride)
        x_high = passed_along(x, "slab", -stride)
        if links:
            d, l, r = update(d, l, r, x_low, x_high, l_low, r_high)
    return last(d, l, r, x_low, x_high)


def solution(mesh):
    return jax.shard_map(
        shards,
        mesh=mesh,
        in_specs=(
            P("slab", None),
            P("slab", None, None),
            P("slab", None),
            P("slab", None, None),
            P("energy"),
            P("energy"),
        ),
        out_specs=(P(("energy", "slab"), None, None), P(("energy", "slab"), None, None)),
        check_vma=False,
    )
```
